128 devices in a mesh: row: 16 (over z, y_lo, core), col: 8 (over y_hi, x).
Axes of the slice: x: 4, y: 4 (y_hi: 2, y_lo: 2; y = y_hi * 2 + y_lo), z: 4, core: 2. Of those that a mesh axis runs over, the one named last changes fastest.
Arguments:
- amplitudes: float32 [256, 1024, 1024], P(None, 'row', 'col'), may hold values from -6 to 6
- int_plus: float32 [256, 1024, 1024], P(None, 'row', 'col'), may hold values from -0.0078125 to 0.0078125
- int_minus: float32 [256, 1024, 1024], P(None, 'row', 'col'), may hold values from -0.0078125 to 0.0078125
Outputs:
- upper_res: float32 [256, 256], P('row', 'col')
- lower_res: float32 [256, 256], P('row', 'col')
The draws below stay inside these ranges and needn't reach their ends.
All inputs are finite; a program needn't handle non-finite values.
Results may differ from the reference program's by a relative error of at most 0.0001.
Values sent between devices are 32-bit elements; how exact they have to be, the bound alone decides.
No kernel may reach another device: no remote copies, remote signals or barrier semaphores. Data moves between devices by JAX's collectives and lax.ppermute only.
A program may use at most 192 MiB of HBM per device.

```python
import jax
import jax.numpy as jnp
from jax import lax

V = 1024
P_SIZE = 256
AB = 256
N_ROW = 16


def spiked(result, own_key, source, target, shards_of, factor):
    owner, partner = [(jnp.arange(result.shape[axis_at]) // (result.shape[axis_at] // shards_of)).reshape([-1 if axis == axis_at else 1 for axis in range(result.ndim)]) for axis_at in (source, target)]
    chosen = jax.random.permutation(own_key, shards_of)[partner]
    strong = (owner == chosen) | (owner == (partner + shards_of // 2) % shards_of)
    return jnp.where(strong, factor * result, result)


def steps_of(key, shape, split, least, top_value):
    loudness, own = 1.0, jax.random.fold_in(key, 6)
    for axis_at, shards_of in split:
        steps = jnp.exp(jax.random.uniform(jax.random.fold_in(own, axis_at), (shards_of,), jnp.float32, least / len(split), top_value / len(split)))
        loudness = loudness * jnp.repeat(steps, shape[axis_at] // shards_of).reshape([-1 if axis == axis_at else 1 for axis in range(len(shape))])
    return loudness


def bell_draw_with(stream_key, extent, scale, bound, cuts, heavy, held_as=jnp.bfloat16):
    result = scale * jax.random.normal(stream_key, extent, jnp.float32)
    if cuts:
        result = result * steps_of(stream_key, extent, cuts, -0.22, 0.18)
    return jnp.clip(spiked(result, jax.random.fold_in(stream_key, 3), *heavy), -bound, bound).astype(held_as)


def setup_inputs(seed: int = 0) -> dict:
    keys = jax.random.split(jax.random.key(seed), 4)
    return {
        "amplitudes": bell_draw_with(keys[0], (P_SIZE, V, V), 1.0, 6.0, ((1, 16), (2, 8)), (2, 0, 8, 2.0), jnp.float32),
        "int_plus": bell_draw_with(keys[1], (AB, V, V), (V * V) ** -0.5, 0.0078125, ((1, 16), (2, 8)), (1, 0, 16, 2.0), jnp.float32),
        "int_minus": bell_draw_with(keys[2], (AB, V, V), (V * V) ** -0.5, 0.0078125, ((1, 16), (2, 8)), (1, 0, 16, 2.0), jnp.float32),
    }


def reference(amplitudes, int_plus, int_minus):
    pairs = amplitudes.shape[0]
    virtuals = amplitudes.shape[1]
    window = int_plus.shape[0]
    block = virtuals // N_ROW

    def step(index, carry):
        acc_sym, acc_anti = carry
        start = (index * block).astype(jnp.int32)
        rows = lax.dynamic_slice_in_dim(amplitudes, start, block, 1)
        columns = lax.dynamic_slice_in_dim(amplitudes, start, block, 2)
        mirror = jnp.transpose(columns, (0, 2, 1))
        c_index = start + lax.broadcasted_iota(jnp.int32, (block, virtuals), 0)
        d_index = lax.broadcasted_iota(jnp.int32, (block, virtuals), 1)
        weight = jnp.where(c_index < d_index, 1.0, jnp.where(c_index == d_index, 0.5, 0.0)).astype(jnp.float32)
        sym = (rows + mirror) * weight
        anti = (rows - mirror) * weight
        plus_block = lax.dynamic_slice_in_dim(int_plus, start, block, 1)
        minus_block = lax.dynamic_slice_in_dim(int_minus, start, block, 1)
        acc_sym = acc_sym + jnp.einsum("qcd,pcd->qp", plus_block, sym, precision=lax.Precision.HIGHEST)
        acc_anti = acc_anti + jnp.einsum("qcd,pcd->qp", minus_block, anti, precision=lax.Precision.HIGHEST)
        return acc_sym, acc_anti

    start_sums = (jnp.zeros((window, pairs), jnp.float32), jnp.zeros((window, pairs), jnp.float32))
    part_sym, part_anti = lax.fori_loop(0, N_ROW, step, start_sums)
    return part_sym + part_anti, part_sym - part_anti
```

```python
import jax
import jax.numpy as jnp
from jax import lax
from jax.experimental import pallas as pl
from jax.experimental.pallas import tpu as pltpu
from jax.sharding import PartitionSpec as P

AXES = ("row", "col")
F32 = jnp.float32
BF16 = jnp.bfloat16

PAIRS, C, D = 256, 64, 128
SENT = 44
KEPT = C - SENT
GROUPS, LOW = 4, 16
ROWS = SENT * LOW
KROWS = KEPT * LOW
PIECE = 88
HALF = GROUPS * ROWS
LOWER, UPPER, DIAG = 0, 1, 2
HBM = pltpu.MemorySpace.HBM


def split(x):
    high = x.astype(BF16)
    return high, (x - high.astype(F32)).astype(BF16)


def product(left, right, dims):
    lh, ll = left
    rh, rl = right

    def dot(a, b):
        return lax.dot_general(a, b, (dims, ((), ())), preferred_element_type=F32)

    return dot(lh, rh) + (dot(lh, rl) + dot(ll, rh))


NT = ((1,), (1,))
NN = ((1,), (0,))


def weight_row(info, c):
    c_index = info[2] + c
    d_index = info[3] + lax.broadcasted_iota(jnp.int32, (1, D), 1)
    return jnp.where(c_index < d_index, 1.0, jnp.where(c_index == d_index, 0.5, 0.0)).astype(F32)


def prepare_kernel(info, amp, plus, minus, msg, kept0, kept1, abuf, wbuf, ibuf, mbuf, sem_in, sem_out):
    role = info[0]
    kept = (kept0, kept1)

    @pl.when(role != UPPER)
    def _():
        loads = [
            pltpu.make_async_copy(amp.at[:, pl.ds(LOW * g, LOW), :], abuf.at[g], sem_in.at[g])
            for g in range(GROUPS)
        ]
        for load in loads:
            load.start()
        stores = []
        for g in range(GROUPS):
            loads[g].wait()
            rows = abuf.at[g].reshape(PAIRS * LOW, D)

            def step(low, carry, rows=rows, g=g):
                turned = rows[pl.ds(low, PAIRS, stride=LOW), :].T
                for u in range(2):
                    for h in range(2):
                        wbuf[u, h, g, pl.ds(low, C, stride=LOW), :] = turned[
                            C * u : C * u + C, D * h : D * h + D
                        ]
                return carry

            lax.fori_loop(0, LOW, step, 0, unroll=2)
            for u in range(2):
                for h in range(2):
                    source = wbuf.at[u, h, g]
                    stores.append(
                        pltpu.make_async_copy(
                            source.at[pl.ds(0, ROWS), :].reshape(8, PIECE, D),
                            msg.at[u, :, h, g],
                            sem_out.at[len(stores)],
                        )
                    )
                    stores.append(
                        pltpu.make_async_copy(
                            source.at[pl.ds(ROWS, KROWS), :], kept[u].at[h, g], sem_out.at[len(stores)]
                        )
                    )
            for store in stores[-8:]:
                store.start()
        for store in stores:
            store.wait()

    @pl.when(role == UPPER)
    def _():
        loads = [
            pltpu.make_async_copy(ref.at[:, pl.ds(C - 24, 24), :], ibuf.at[i], sem_in.at[i])
            for i, ref in enumerate((plus, minus))
        ]
        for load in loads:
            load.start()
        for l in range(2):
            for h in range(2):
                mbuf[l, h, pl.ds(2 * GROUPS * KROWS, HALF - 2 * GROUPS * KROWS), :] = jnp.zeros(
                    (HALF - 2 * GROUPS * KROWS, D), F32
                )
        for i in range(2):
            loads[i].wait()
            rows = ibuf.at[i].reshape(PAIRS * 24, D)

            def step(c, carry, rows=rows, i=i):
                turned = rows[pl.ds(24 - KEPT + c, PAIRS, stride=24), :].T
                for l in range(2):
                    for h in range(2):
                        for g in range(GROUPS):
                            at = pl.multiple_of((i * GROUPS + g) * KROWS + c * LOW, LOW)
                            mbuf[l, h, pl.ds(at, LOW), :] = turned[
                                C * l + LOW * g : C * l + LOW * g + LOW, D * h : D * h + D
                            ]
                return carry

            lax.fori_loop(0, KEPT, step, 0, unroll=2)
        stores = []
        for l in range(2):
            for h in range(2):
                for g in range(GROUPS):
                    stores.append(
                        pltpu.make_async_copy(
                            mbuf.at[l, h, pl.ds(ROWS * g, ROWS), :].reshape(8, PIECE, D),
                            msg.at[l, :, h, g],
                            sem_out.at[len(stores)],
                        )
                    )
        for store in stores:
            store.start()
        for store in stores:
            store.wait()


def own_kernel(info, plus, minus, amp, kept0, kept1, cross, sym, anti):
    role, core, block = info[0], info[1], pl.program_id(0)

    @pl.when(block == 0)
    def _():
        sym[...] = jnp.zeros_like(sym)
        anti[...] = jnp.zeros_like(anti)

    def taken(ref, low, weighted):
        part = ref.reshape(PAIRS * 8, D)[pl.ds(low, PAIRS, stride=8), :]
        return part * weight_row(info, block * 8 + low) if weighted else part

    @pl.when(role != LOWER)
    def _():
        right = split(jnp.concatenate([taken(amp, low, False) for low in range(8)], axis=1))
        for ref, out in ((plus, sym), (minus, anti)):
            left = split(jnp.concatenate([taken(ref, low, True) for low in range(8)], axis=1))
            out[...] += product(left, right, NT)

    for low in range(8):
        c = block * 8 + low

        @pl.when((role == DIAG) & (c >= SENT))
        def _(low=low, c=c):
            at = pl.multiple_of((c - SENT) * LOW, LOW)

            def rows_of(ref):
                return jnp.concatenate(
                    [
                        jnp.concatenate([ref[h, g, pl.ds(at, LOW), :] for g in range(GROUPS)], axis=0)
                        for h in range(2)
                    ],
                    axis=1,
                )

            first = jnp.where(core == 0, rows_of(kept0), 0.0)
            second = jnp.where(core == 0, rows_of(cross), rows_of(kept1))
            right = split(jnp.concatenate([first, second], axis=0))
            sym[...] += product(split(taken(plus, low, True)), right, NN)
            anti[...] -= product(split(taken(minus, low, True)), right, NN)


def mirror_kernel(info, sym, anti, plus, minus, got, kept0, kept1, out, ibuf, gbuf, kbuf, res, sem_i, sem_g):
    role = info[0]
    gets = [
        pltpu.make_async_copy(got.at[k, h], gbuf.at[k, h], sem_g.at[2 * k + h]) for k in range(2) for h in range(2)
    ]
    for get in gets:
        get.start()
    res[0] = sym[...]
    res[1] = anti[...]
    blocks = (SENT + 7) // 8

    @pl.when(role != LOWER)
    def _():
        loads = [
            [
                pltpu.make_async_copy(ref.at[:, pl.ds(8 * j, 8), :], ibuf.at[i, j], sem_i.at[i, j])
                for i, ref in enumerate((plus, minus))
            ]
            for j in range(blocks)
        ]
        for pair in loads:
            for load in pair:
                load.start()
        for get in gets:
            get.wait()
        for j in range(blocks):
            lows = range(min(8, SENT - 8 * j))
            right = split(
                jnp.concatenate(
                    [
                        jnp.concatenate(
                            [
                                gbuf[k, h, pl.ds(g * ROWS + (8 * j + low) * LOW, LOW), :]
                                for low in lows
                                for k in range(2)
                                for g in range(GROUPS)
                            ],
                            axis=0,
                        )
                        for h in range(2)
                    ],
                    axis=1,
                )
            )
            for i in range(2):
                loads[j][i].wait()
                rows = ibuf.at[i, j].reshape(PAIRS * 8, D)
                left = split(
                    jnp.concatenate(
                        [
                            rows[pl.ds(low, PAIRS, stride=8), :] * weight_row(info, 8 * j + low)
                            for low in lows
                        ],
                        axis=1,
                    )
                )
                part = product(left, right, NN)
                res[i] = res[i] + part if i == 0 else res[i] - part

    @pl.when(role == LOWER)
    def _():
        loads = [
            pltpu.make_async_copy(ref, kbuf.at[k], sem_i.at[k, 0]) for k, ref in enumerate((kept0, kept1))
        ]
        for load in loads:
            load.start()
        for get in gets:
            get.wait()
        count = GROUPS * KROWS
        for k in range(2):
            loads[k].wait()
            right = split(
                jnp.concatenate([kbuf[k, h].reshape(count, D) for h in range(2)], axis=1)
            )
            for i in range(2):
                left = jnp.concatenate(
                    [gbuf[k, h, pl.ds(i * count, count), :].T for h in range(2)], axis=0
                )
                part = product(split(left), right, NN)
                res[i] = res[i] + part if i == 0 else res[i] - part

    both = res[0] + res[1], res[0] - res[1]
    res[0] = both[0]
    res[1] = both[1]
    lane = lax.broadcasted_iota(jnp.int32, (8, D), 1) // 32

    def pack(r, carry):
        at = pl.multiple_of(r * 16, 16)
        parts = [res[o, pl.ds(at + 8 * f if f else at, 8), :] for o in range(2) for f in range(2)]
        for k in range(8):
            tile = None
            for g in range(4):
                x = parts[g][:, D * (k // 4) : D * (k // 4) + D]
                shift = (32 * g - 32 * (k % 4)) % D
                x = pltpu.roll(x, shift, 1) if shift else x
                tile = x if tile is None else jnp.where(lane == g, x, tile)
            out[r * 8 + k] = tile
        return carry

    lax.fori_loop(0, 16, pack, 0)


def sum_kernel(parts, upper, lower):
    total = jnp.sum(parts[...], axis=0)
    for g, ref in enumerate((upper, upper, lower, lower)):
        ref[8 * (g % 2) : 8 * (g % 2) + 8, :] = total[:, 32 * g : 32 * g + 32]


def whole(shape):
    return pl.BlockSpec(shape, lambda *_: (0,) * len(shape))


ANY = pl.BlockSpec(memory_space=HBM)
SCALARS = pl.BlockSpec(memory_space=pltpu.SMEM)


def device(row_chip, core, col):
    return (row_chip * 2 + core) * 8 + col


def body(amplitudes, int_plus, int_minus):
    row, col = lax.axis_index("row"), lax.axis_index("col")
    chip, core = row // 2, row % 2
    role = jnp.where(chip > col, LOWER, jnp.where(chip < col, UPPER, DIAG))
    info = jnp.stack([role, core, row * C, col * D]).astype(jnp.int32)

    msg, kept0, kept1 = pl.pallas_call(
        prepare_kernel,
        in_specs=[SCALARS, ANY, ANY, ANY],
        out_specs=[ANY, ANY, ANY],
        out_shape=[
            jax.ShapeDtypeStruct((2, 8, 2, GROUPS, PIECE, D), F32),
            jax.ShapeDtypeStruct((2, GROUPS, KROWS, D), F32),
            jax.ShapeDtypeStruct((2, GROUPS, KROWS, D), F32),
        ],
        scratch_shapes=[
            pltpu.VMEM((GROUPS, PAIRS, LOW, D), F32),
            pltpu.VMEM((2, 2, GROUPS, C * LOW, D), F32),
            pltpu.VMEM((2, PAIRS, 24, D), F32),
            pltpu.VMEM((2, 2, HALF, D), F32),
            pltpu.SemaphoreType.DMA((GROUPS,)),
            pltpu.SemaphoreType.DMA((32,)),
        ],
        name="prepare",
    )(info, amplitudes, int_plus, int_minus)

    chips = [(r, k) for r in range(8) for k in range(8)]
    first_order = [[device(r, u, k) for u in range(2) for r, k in chips]]
    second_order = [[device(k, u, r) for r, k in chips] for u in range(2)]
    spread = lax.all_to_all(
        msg.reshape(128, PIECE, D), AXES, 0, 0, tiled=True, axis_index_groups=first_order
    )
    got = lax.all_to_all(
        spread.reshape(2, 64, PIECE, D), AXES, 1, 1, tiled=True, axis_index_groups=second_order
    )
    cross = lax.ppermute(kept0, AXES, [(device(r, 1, r), device(r, 0, r)) for r in range(8)])

    block = pl.BlockSpec((PAIRS, 8, D), lambda j: (0, j, 0))
    kept_block = whole((2, GROUPS, KROWS, D))
    sym, anti = pl.pallas_call(
        own_kernel,
        grid=(C // 8,),
        in_specs=[SCALARS, block, block, block, kept_block, kept_block, kept_block],
        out_specs=[whole((PAIRS, PAIRS))] * 2,
        out_shape=[jax.ShapeDtypeStruct((PAIRS, PAIRS), F32)] * 2,
        compiler_params=pltpu.CompilerParams(dimension_semantics=("arbitrary",)),
        name="own",
    )(info, int_plus, int_minus, amplitudes, kept0, kept1, cross)

    packed = pl.pallas_call(
        mirror_kernel,
        in_specs=[SCALARS, whole((PAIRS, PAIRS)), whole((PAIRS, PAIRS)), ANY, ANY, ANY, ANY, ANY],
        out_specs=whole((128, 8, D)),
        out_shape=jax.ShapeDtypeStruct((128, 8, D), F32),
        scratch_shapes=[
            pltpu.VMEM((2, (SENT + 7) // 8, PAIRS, 8, D), F32),
            pltpu.VMEM((2, 2, HALF, D), F32),
            pltpu.VMEM((2, 2, GROUPS, KROWS, D), F32),
            pltpu.VMEM((2, PAIRS, PAIRS), F32),
            pltpu.SemaphoreType.DMA((2, (SENT + 7) // 8)),
            pltpu.SemaphoreType.DMA((4,)),
        ],
        name="mirror",
    )(info, sym, anti, int_plus, int_minus, got.reshape(2, 2, HALF, D), kept0, kept1)

    parts = lax.all_to_all(packed, AXES, 0, 0, tiled=True)
    return pl.pallas_call(
        sum_kernel,
        in_specs=[whole((128, 8, D))],
        out_specs=[whole((16, 32))] * 2,
        out_shape=[jax.ShapeDtypeStruct((16, 32), F32)] * 2,
        grid=(1,),
        name="total",
    )(parts)


def solution(mesh):
    spec = P(None, "row", "col")
    out = (P("row", "col"), P("row", "col"))
    return jax.shard_map(body, mesh=mesh, in_specs=(spec,) * 3, out_specs=out, check_vma=False)
```

```python
from functools import partial

import jax
import jax.numpy as jnp
from jax import lax
from jax.experimental import pallas as pl
from jax.experimental.pallas import tpu as pltpu
from jax.sharding import PartitionSpec as P

AXES = ("row", "col")
F32 = jnp.float32
BF16 = jnp.bfloat16


PAIRS, C, D = 256, 64, 128
CHUNKS, WINDOW = 4, 16
SENT, KEPT = 11, 5
GROUPS, LOW = 4, 16
SROWS, KROWS = SENT * LOW, KEPT * LOW
HALF = GROUPS * SROWS
LOWER, UPPER, DIAG = 0, 1, 2
OWN = (((0, 4), 0), ((4, 8), 4))
HBM = pltpu.MemorySpace.HBM

ROUTES = (
    (
        16, 40, 27, 100, 49, 105, 99, 26, 3, 43, 84, 101, 107, 15, 20, 10, 50, 64, 68, 29, 122, 12, 57, 59,
        96, 77, 22, 124, 32, 25, 51, 63, 81, 102, 113, 11, 17, 58, 75, 37, 82, 103, 48, 18, 42, 93, 66, 126,
        71, 8, 39, 33, 95, 94, 30, 67, 41, 1, 46, 74, 69, 110, 115, 52, 61, 53, 55, 86, 108, 119, 56, 120, 38,
        44, 79, 70, 118, 4, 45, 90, 72, 73, 106, 125, 0, 9, 65, 34, 89, 78, 116, 112, 21, 2, 23, 121, 87, 127,
        123, 104, 91, 19, 76, 117, 111, 24, 98, 6, 35, 92, 85, 109,
    ),
    (
        25, 97, 19, 47, 121, 122, 115, 9, 33, 58, 112, 44, 98, 108, 8, 18, 7, 84, 101, 106, 6, 16, 42, 48, 63,
        117, 125, 4, 10, 41, 56, 52, 88, 82, 15, 3, 21, 67, 64, 38, 74, 83, 27, 57, 43, 65, 90, 95, 11, 12,
        26, 89, 87, 69, 110, 96, 104, 32, 54, 55, 81, 71, 116, 20, 105, 39, 40, 92, 113, 103, 37, 1, 45, 62,
        76, 78, 99, 120, 49, 46, 60, 36, 118, 127, 123, 31, 13, 35, 79, 77, 126, 5, 2, 50, 75, 70, 86, 107,
        100, 28, 14, 80, 124, 94, 111, 24, 29, 59, 23, 72, 93, 109,
    ),
    (
        21, 33, 59, 116, 39, 102, 111, 24, 42, 55, 76, 45, 22, 112, 9, 35, 48, 85, 105, 117, 123, 3, 10, 27,
        53, 65, 127, 122, 28, 13, 47, 84, 80, 70, 7, 40, 2, 62, 68, 69, 93, 79, 4, 57, 46, 63, 29, 124, 83, 1,
        5, 32, 60, 88, 74, 119, 56, 61, 50, 43, 77, 82, 99, 96, 17, 71, 64, 92, 126, 115, 26, 41, 89, 67, 94,
        103, 72, 51, 49, 90, 34, 52, 101, 104, 12, 30, 18, 0, 100, 125, 118, 8, 106, 58, 66, 108, 109, 114,
        20, 25, 15, 19, 78, 86, 110, 16, 97, 81, 11, 87, 95, 98,
    ),
    (
        13, 62, 56, 104, 113, 29, 115, 28, 40, 43, 45, 120, 127, 100, 1, 46, 38, 52, 101, 106, 103, 12, 49,
        58, 94, 61, 118, 107, 2, 41, 50, 53, 89, 126, 70, 9, 16, 63, 73, 78, 6, 91, 24, 19, 42, 64, 36, 23,
        31, 8, 18, 35, 60, 37, 86, 71, 44, 11, 90, 39, 93, 109, 108, 32, 33, 81, 75, 117, 111, 87, 123, 112,
        59, 55, 92, 110, 95, 26, 25, 57, 54, 69, 125, 124, 15, 97, 74, 10, 76, 65, 116, 5, 21, 30, 3, 79, 77,
        7, 27, 14, 122, 47, 80, 72, 98, 4, 22, 82, 48, 83, 84, 99,
    ),
    (
        17, 35, 27, 87, 89, 113, 108, 1, 41, 40, 44, 109, 22, 112, 32, 90, 123, 53, 66, 6, 4, 24, 42, 48, 84,
        45, 125, 111, 8, 25, 51, 5, 117, 31, 71, 11, 57, 26, 86, 38, 126, 79, 16, 49, 34, 124, 70, 98, 7, 3,
        18, 43, 67, 60, 23, 103, 19, 97, 82, 72, 37, 39, 15, 96, 21, 65, 52, 93, 100, 119, 0, 121, 14, 56, 68,
        110, 118, 120, 9, 46, 54, 116, 101, 94, 105, 33, 30, 99, 69, 85, 95, 13, 2, 58, 75, 76, 61, 127, 115,
        106, 50, 55, 92, 77, 78, 12, 10, 91, 59, 28, 29, 102,
    ),
    (
        25, 11, 35, 4, 76, 117, 15, 97, 66, 59, 84, 36, 30, 115, 45, 2, 114, 124, 89, 106, 122, 104, 82, 26,
        40, 29, 22, 28, 41, 49, 83, 80, 38, 126, 110, 19, 57, 43, 113, 78, 47, 6, 96, 120, 75, 60, 37, 95, 99,
        8, 16, 10, 72, 65, 94, 87, 48, 73, 31, 32, 77, 79, 7, 24, 53, 54, 67, 61, 125, 116, 112, 105, 90, 81,
        52, 70, 92, 121, 9, 18, 62, 69, 109, 127, 1, 98, 74, 42, 108, 101, 111, 12, 21, 50, 3, 123, 93, 118,
        56, 33, 46, 55, 71, 86, 14, 44, 5, 58, 27, 100, 20, 103,
    ),
    (
        25, 53, 75, 112, 76, 124, 39, 16, 48, 91, 84, 37, 114, 79, 1, 42, 58, 61, 109, 70, 108, 24, 10, 50,
        117, 77, 97, 104, 11, 65, 59, 47, 89, 126, 7, 33, 2, 43, 63, 81, 86, 123, 40, 18, 34, 72, 105, 62,
        127, 56, 9, 82, 87, 101, 110, 31, 28, 8, 49, 3, 93, 38, 111, 80, 0, 113, 107, 85, 121, 119, 57, 17,
        74, 64, 125, 78, 95, 32, 41, 45, 55, 60, 118, 100, 51, 22, 26, 67, 71, 69, 15, 99, 106, 90, 35, 36,
        94, 30, 19, 13, 83, 66, 103, 92, 23, 27, 120, 6, 115, 68, 116, 102,
    ),
    (
        1, 99, 59, 108, 13, 27, 115, 49, 3, 56, 52, 109, 98, 12, 121, 33, 44, 64, 69, 106, 53, 104, 2, 19, 92,
        93, 29, 107, 9, 25, 90, 91, 113, 78, 110, 112, 105, 50, 72, 45, 6, 15, 88, 58, 42, 23, 54, 22, 71, 8,
        89, 32, 60, 66, 126, 7, 16, 96, 41, 55, 77, 70, 87, 4, 40, 63, 35, 95, 111, 116, 24, 97, 38, 48, 76,
        14, 39, 36, 5, 57, 75, 80, 86, 30, 28, 65, 74, 10, 101, 125, 103, 124, 21, 26, 31, 37, 61, 127, 79,
        81, 83, 43, 84, 94, 118, 120, 11, 18, 67, 100, 117, 122,
    ),
)


def split(x):
    high = x.astype(BF16)
    return high, (x - high.astype(F32)).astype(BF16)


def product(left, right, dims):
    lh, ll = left
    rh, rl = right

    def dot(a, b):
        return lax.dot_general(a, b, (dims, ((), ())), preferred_element_type=F32)

    return dot(lh, rh) + (dot(lh, rl) + dot(ll, rh))


NT = ((1,), (1,))
NN = ((1,), (0,))


def weight_row(info, c):
    c_index = info[2] + c
    d_index = info[3] + lax.broadcasted_iota(jnp.int32, (1, D), 1)
    return jnp.where(c_index < d_index, 1.0, jnp.where(c_index == d_index, 0.5, 0.0)).astype(F32)


def prepare_kernel(info, amp, plus, minus, *refs):
    slots, (kept0, kept1) = refs[: 2 * CHUNKS], refs[2 * CHUNKS : 2 * CHUNKS + 2]
    abuf, wbuf, ibuf, mbuf, sem_in, sem_out = refs[2 * CHUNKS + 2 :]
    role, core = info[0], info[1]

    @pl.when(role != UPPER)
    def _():
        loads = [
            pltpu.make_async_copy(amp.at[:, pl.ds(LOW * g, LOW), :], abuf.at[g], sem_in.at[g])
            for g in range(GROUPS)
        ]
        for load in loads:
            load.start()
        stores = []
        for g in range(GROUPS):
            loads[g].wait()
            rows = abuf.at[g].reshape(PAIRS * LOW, D)

            def step(low, carry, rows=rows, g=g):
                turned = rows[pl.ds(low, PAIRS, stride=LOW), :].T
                for u in range(2):
                    for h in range(2):
                        wbuf[u, h, g, pl.ds(low, C, stride=LOW), :] = turned[
                            C * u : C * u + C, D * h : D * h + D
                        ]
                return carry

            lax.fori_loop(0, LOW, step, 0, unroll=2)
            first = len(stores)
            for j in range(CHUNKS):
                for t in range(2):
                    stores.append(
                        pltpu.make_async_copy(
                            wbuf.at[core ^ t, :, g, pl.ds(WINDOW * LOW * j, SROWS), :],
                            slots[2 * j + t].at[:, pl.ds(SROWS * g, SROWS), :],
                            sem_out.at[len(stores)],
                        )
                    )
                for u, kept in enumerate((kept0, kept1)):
                    stores.append(
                        pltpu.make_async_copy(
                            wbuf.at[u, :, g, pl.ds(WINDOW * LOW * j + SROWS, KROWS), :],
                            kept.at[:, j, g],
                            sem_out.at[len(stores)],
                        )
                    )
            for store in stores[first:]:
                store.start()
        for store in stores:
            store.wait()

    @pl.when(role == UPPER)
    def _():
        loads = [
            [
                pltpu.make_async_copy(
                    ref.at[:, pl.ds(WINDOW * j + 8, 8), :], ibuf.at[i, j], sem_in.at[CHUNKS * i + j]
                )
                for i, ref in enumerate((plus, minus))
            ]
            for j in range(CHUNKS)
        ]
        for pair in loads:
            for load in pair:
                load.start()
        used = 2 * GROUPS * KROWS
        stores = []
        for j in range(CHUNKS):
            for i in range(2):
                loads[j][i].wait()
                rows = ibuf.at[i, j].reshape(PAIRS * 8, D)
                for c in range(KEPT):
                    turned = rows[pl.ds(8 - KEPT + c, PAIRS, stride=8), :].T
                    for l in range(2):
                        for h in range(2):
                            for g in range(GROUPS):
                                mbuf[l, j, h, pl.ds((i * GROUPS + g) * KROWS + c * LOW, LOW), :] = turned[
                                    C * l + LOW * g : C * l + LOW * g + LOW, D * h : D * h + D
                                ]
            for l in range(2):
                for h in range(2):
                    mbuf[l, j, h, pl.ds(used, HALF - used), :] = jnp.zeros((HALF - used, D), F32)
            for t in range(2):
                store = pltpu.make_async_copy(mbuf.at[core ^ t, j], slots[2 * j + t], sem_out.at[len(stores)])
                store.start()
                stores.append(store)
        for store in stores:
            store.wait()


def own_kernel(start, info, plus, minus, amp, kept0, kept1, cross, *refs):
    sym, anti = refs[-2:]
    role, core, block = info[0], info[1], pl.program_id(0) + start

    @pl.when(block == start)
    def _():
        for ref, i in ((sym, 0), (anti, 1)):
            ref[...] = refs[i][...] if start else jnp.zeros_like(ref)

    def taken(ref, low, weighted):
        part = ref.reshape(PAIRS * 8, D)[pl.ds(low, PAIRS, stride=8), :]
        return part * weight_row(info, block * 8 + low) if weighted else part

    @pl.when(role != LOWER)
    def _():
        right = split(jnp.concatenate([taken(amp, low, False) for low in range(8)], axis=1))
        for ref, out in ((plus, sym), (minus, anti)):
            left = split(jnp.concatenate([taken(ref, low, True) for low in range(8)], axis=1))
            out[...] += product(left, right, NT)

    @pl.when((role == DIAG) & (block % 2 == 1))
    def _():
        def rows_of(ref, h, c):
            return [ref[h, 0, g, pl.ds(c * LOW, LOW), :] for g in range(GROUPS)]

        rights = []
        for h in range(2):
            pieces = []
            for c in range(KEPT):
                first = jnp.concatenate(rows_of(kept0, h, c), axis=0)
                pieces.append(jnp.where(core == 0, first, 0.0))
                theirs = jnp.concatenate(rows_of(cross, h, c), axis=0)
                pieces.append(jnp.where(core == 0, theirs, jnp.concatenate(rows_of(kept1, h, c), axis=0)))
            rights.append(jnp.concatenate(pieces, axis=0))
        right = split(jnp.concatenate(rights, axis=1))
        lows = range(8 - KEPT, 8)
        for ref, out, sign in ((plus, sym, 1.0), (minus, anti, -1.0)):
            left = split(jnp.concatenate([taken(ref, low, True) for low in lows], axis=1))
            out[...] += sign * product(left, right, NN)


def mirror_kernel(chunk, info, sym, anti, plus, minus, same, other, own, kept0, kept1, *refs):
    outs, (ibuf, gbuf, kbuf, res, sem_i, sem_g) = refs[:-6], refs[-6:]
    role, core = info[0], info[1]
    res[0] = sym[...]
    res[1] = anti[...]
    other_get = pltpu.make_async_copy(other, gbuf.at[1], sem_g.at[1])
    other_get.start()

    @pl.when(role == DIAG)
    def _():
        pltpu.make_async_copy(own, gbuf.at[0], sem_g.at[0]).start()

    @pl.when(role != DIAG)
    def _():
        pltpu.make_async_copy(same, gbuf.at[0], sem_g.at[0]).start()

    same_get = pltpu.make_async_copy(same, gbuf.at[0], sem_g.at[0])

    @pl.when(role != LOWER)
    def _():
        loads = [
            pltpu.make_async_copy(ref.at[:, pl.ds(WINDOW * chunk, WINDOW), :], ibuf.at[i], sem_i.at[i])
            for i, ref in enumerate((plus, minus))
        ]
        for load in loads:
            load.start()
        same_get.wait()
        other_get.wait()
        rights = []
        for h in range(2):
            pieces = []
            for c in range(SENT):
                for l in range(2):
                    for g in range(GROUPS):
                        pieces.append(gbuf[core ^ l, h, pl.ds(g * SROWS + c * LOW, LOW), :])
            rights.append(jnp.concatenate(pieces, axis=0))
        right = split(jnp.concatenate(rights, axis=1))
        for i in range(2):
            loads[i].wait()
            rows = ibuf.at[i].reshape(PAIRS * WINDOW, D)
            left = split(
                jnp.concatenate(
                    [
                        rows[pl.ds(c, PAIRS, stride=WINDOW), :] * weight_row(info, WINDOW * chunk + c)
                        for c in range(SENT)
                    ],
                    axis=1,
                )
            )
            part = product(left, right, NN)
            res[i] = res[i] + part if i == 0 else res[i] - part

    @pl.when(role == LOWER)
    def _():
        loads = [
            pltpu.make_async_copy(ref.at[:, chunk], kbuf.at[u], sem_i.at[u])
            for u, ref in enumerate((kept0, kept1))
        ]
        for load in loads:
            load.start()
        same_get.wait()
        other_get.wait()
        for load in loads:
            load.wait()
        count = GROUPS * KROWS
        right = split(
            jnp.concatenate(
                [
                    jnp.concatenate([kbuf[core ^ t, h].reshape(count, D) for t in range(2)], axis=0)
                    for h in range(2)
                ],
                axis=1,
            )
        )
        for i in range(2):
            left = jnp.concatenate(
                [
                    jnp.concatenate([gbuf[t, h, pl.ds(i * count, count), :] for t in range(2)], axis=0).T
                    for h in range(2)
                ],
                axis=0,
            )
            part = product(split(left), right, NN)
            res[i] = res[i] + part if i == 0 else res[i] - part

    if chunk < CHUNKS - 1:
        outs[0][...] = res[0]
        outs[1][...] = res[1]
    else:
        pack_parts(res, outs[0])


def pack_parts(res, out):
    both = res[0] + res[1], res[0] - res[1]
    res[0] = both[0]
    res[1] = both[1]
    lane = lax.broadcasted_iota(jnp.int32, (8, D), 1) // 32

    def pack(r, carry):
        at = pl.multiple_of(r * 16, 16)
        parts = [res[o, pl.ds(at + 8 * f if f else at, 8), :] for o in range(2) for f in range(2)]
        for k in range(8):
            tile = None
            for g in range(4):
                x = parts[g][:, D * (k // 4) : D * (k // 4) + D]
                shift = (32 * g - 32 * (k % 4)) % D
                x = pltpu.roll(x, shift, 1) if shift else x
                tile = x if tile is None else jnp.where(lane == g, x, tile)
            out[r * 8 + k] = tile
        return carry

    lax.fori_loop(0, 16, pack, 0)


def sum_kernel(parts, upper, lower):
    total = jnp.sum(parts[...], axis=0)
    for g, ref in enumerate((upper, upper, lower, lower)):
        ref[8 * (g % 2) : 8 * (g % 2) + 8, :] = total[:, 32 * g : 32 * g + 32]


def whole(shape):
    return pl.BlockSpec(shape, lambda *_: (0,) * len(shape))


ANY = pl.BlockSpec(memory_space=HBM)
SCALARS = pl.BlockSpec(memory_space=pltpu.SMEM)


def device(row_chip, core, col):
    return (row_chip * 2 + core) * 8 + col


def legs(slot):
    chips = [(r, k) for r in range(8) for k in range(8)]
    senders = sorted(device(r, u, k) for r, k in chips if r != k for u in range(2))
    first, second = [], []
    for source, via in zip(senders, ROUTES[slot]):
        chip, core, col = source // 16, source // 8 % 2, source % 8
        first.append((source, via))
        second.append((via, device(col, core ^ (slot % 2), chip)))
    if slot % 2:
        inside = [(device(r, 1, r), device(r, 0, r)) for r in range(8)]
        first += inside
        second += [(b, b) for _, b in inside]
    return first, second


def body(amplitudes, int_plus, int_minus):
    row, col = lax.axis_index("row"), lax.axis_index("col")
    chip, core = row // 2, row % 2
    role = jnp.where(chip > col, LOWER, jnp.where(chip < col, UPPER, DIAG))
    info = jnp.stack([role, core, row * C, col * D]).astype(jnp.int32)

    slot_shape = jax.ShapeDtypeStruct((2, HALF, D), F32)
    kept_shape = jax.ShapeDtypeStruct((2, CHUNKS, GROUPS, KROWS, D), F32)
    *slots, kept0, kept1 = pl.pallas_call(
        prepare_kernel,
        in_specs=[SCALARS, ANY, ANY, ANY],
        out_specs=[ANY] * (2 * CHUNKS + 2),
        out_shape=[slot_shape] * (2 * CHUNKS) + [kept_shape] * 2,
        scratch_shapes=[
            pltpu.VMEM((GROUPS, PAIRS, LOW, D), F32),
            pltpu.VMEM((2, 2, GROUPS, C * LOW, D), F32),
            pltpu.VMEM((2, CHUNKS, PAIRS, 8, D), F32),
            pltpu.VMEM((2, CHUNKS, 2, HALF, D), F32),
            pltpu.SemaphoreType.DMA((2 * CHUNKS,)),
            pltpu.SemaphoreType.DMA((64,)),
        ],
        name="prepare",
    )(info, amplitudes, int_plus, int_minus)

    ways = [legs(slot) for slot in range(2 * CHUNKS)]
    passing = [lax.ppermute(x, AXES, way[0]) for x, way in zip(slots, ways)]
    cross = lax.ppermute(kept0, AXES, [(device(r, 1, r), device(r, 0, r)) for r in range(8)])
    square = jax.ShapeDtypeStruct((PAIRS, PAIRS), F32)

    def own_part(start, stop, plus, sums):
        def at(j, info):
            return jnp.where(info[0] == LOWER, 0, j + start)

        block = pl.BlockSpec((PAIRS, 8, D), lambda j, info: (0, at(j, info), 0))
        kept_block = pl.BlockSpec(
            (2, 1, GROUPS, KROWS, D),
            lambda j, info: (0, jnp.where(info[0] == DIAG, (j + start) // 2, 0), 0, 0, 0),
        )
        return pl.pallas_call(
            partial(own_kernel, start),
            grid_spec=pltpu.PrefetchScalarGridSpec(
                num_scalar_prefetch=1,
                grid=(stop - start,),
                in_specs=[block] * 3 + [kept_block] * 3 + [whole((PAIRS, PAIRS))] * len(sums),
                out_specs=[whole((PAIRS, PAIRS))] * 2,
            ),
            out_shape=[square] * 2,
            compiler_params=pltpu.CompilerParams(dimension_semantics=("arbitrary",)),
            name=f"own{start}",
        )(info, plus, int_minus, amplitudes, kept0, kept1, cross, *sums)

    sums = ()
    for (start, stop), slot in OWN:
        plus = lax.optimization_barrier((int_plus, passing[slot - 1]))[0] if slot else int_plus
        sums = own_part(start, stop, plus, sums)
        for s in range(slot, 2 * CHUNKS):
            passing[s] = lax.optimization_barrier((passing[s], sums[0]))[0]
    sym, anti = sums
    got = [lax.ppermute(x, AXES, way[1]) for x, way in zip(passing, ways)]

    for chunk in range(CHUNKS):
        last = chunk == CHUNKS - 1
        packed = jax.ShapeDtypeStruct((128, 8, D), F32)
        out = pl.pallas_call(
            partial(mirror_kernel, chunk),
            in_specs=[SCALARS, whole((PAIRS, PAIRS)), whole((PAIRS, PAIRS))] + [ANY] * 7,
            out_specs=[whole((128, 8, D))] if last else [whole((PAIRS, PAIRS))] * 2,
            out_shape=[packed] if last else [square] * 2,
            scratch_shapes=[
                pltpu.VMEM((2, PAIRS, WINDOW, D), F32),
                pltpu.VMEM((2, 2, HALF, D), F32),
                pltpu.VMEM((2, 2, GROUPS, KROWS, D), F32),
                pltpu.VMEM((2, PAIRS, PAIRS), F32),
                pltpu.SemaphoreType.DMA((2,)),
                pltpu.SemaphoreType.DMA((2,)),
            ],
            name=f"mirror{chunk}",
        )(
            info, sym, anti, int_plus, int_minus,
            got[2 * chunk], got[2 * chunk + 1], slots[2 * chunk], kept0, kept1,
        )
        if not last:
            sym, anti = out

    parts = lax.all_to_all(out[0], AXES, 0, 0, tiled=True)
    return pl.pallas_call(
        sum_kernel,
        in_specs=[whole((128, 8, D))],
        out_specs=[whole((16, 32))] * 2,
        out_shape=[jax.ShapeDtypeStruct((16, 32), F32)] * 2,
        grid=(1,),
        name="total",
    )(parts)


def solution(mesh):
    spec = P(None, "row", "col")
    out = (P("row", "col"), P("row", "col"))
    return jax.shard_map(body, mesh=mesh, in_specs=(spec,) * 3, out_specs=out, check_vma=False)
```

```python
from functools import partial

import jax
import jax.numpy as jnp
from jax import lax
from jax.experimental import pallas as pl
from jax.experimental.pallas import tpu as pltpu
from jax.sharding import PartitionSpec as P

AXES = ("row", "col")
F32 = jnp.float32
BF16 = jnp.bfloat16


PAIRS, C, D = 256, 64, 128
CHUNKS, WINDOW = 4, 16
SENT, KEPT = 11, 5
GROUPS, LOW = 4, 16
SROWS, KROWS = SENT * LOW, KEPT * LOW
HALF = GROUPS * SROWS
LOWER, UPPER, DIAG = 0, 1, 2
MIRROR = ((0, 1), (2, 3))
OWN = (((0, 5), 0), ((5, 8), 4))
HBM = pltpu.MemorySpace.HBM

ROUTES = (
    (
        19, 40, 59, 37, 113, 30, 100, 17, 10, 55, 80, 46, 31, 99, 3, 38, 51, 92, 29, 126, 110, 112, 58, 4,
        106, 68, 122, 15, 33, 25, 50, 63, 45, 94, 91, 8, 57, 56, 88, 70, 119, 121, 9, 18, 43, 95, 76, 127,
        107, 24, 26, 42, 75, 89, 74, 1, 48, 0, 90, 32, 81, 102, 108, 96, 41, 47, 35, 86, 103, 125, 16, 5, 49,
        34, 84, 78, 67, 123, 61, 62, 64, 72, 117, 87, 115, 13, 22, 2, 79, 101, 116, 114, 11, 82, 60, 71, 69,
        109, 28, 98, 6, 7, 77, 93, 111, 120, 20, 14, 27, 124, 85, 118,
    ),
    (
        5, 40, 38, 71, 90, 120, 123, 10, 42, 3, 93, 109, 127, 111, 9, 11, 18, 52, 125, 107, 28, 1, 62, 47, 96,
        101, 118, 103, 20, 19, 55, 79, 89, 6, 7, 2, 13, 54, 39, 48, 126, 82, 12, 57, 46, 74, 37, 22, 75, 32,
        56, 58, 72, 77, 86, 104, 60, 33, 67, 95, 81, 78, 115, 25, 105, 50, 63, 65, 83, 100, 27, 61, 45, 43,
        92, 117, 116, 14, 121, 49, 44, 69, 122, 98, 24, 97, 30, 66, 70, 73, 124, 15, 21, 41, 23, 76, 94, 99,
        16, 4, 80, 35, 64, 87, 110, 112, 8, 26, 59, 108, 84, 106,
    ),
    (
        17, 41, 35, 116, 79, 121, 4, 24, 34, 50, 124, 68, 114, 123, 0, 26, 56, 97, 81, 98, 22, 28, 62, 57, 64,
        69, 30, 120, 8, 2, 40, 73, 93, 102, 108, 3, 1, 59, 85, 90, 13, 83, 16, 49, 43, 60, 80, 29, 20, 19, 27,
        33, 87, 70, 31, 103, 32, 9, 53, 94, 84, 109, 127, 44, 99, 54, 52, 37, 110, 63, 48, 112, 36, 47, 88,
        111, 106, 18, 72, 46, 51, 77, 126, 119, 5, 10, 58, 75, 100, 71, 118, 12, 21, 74, 42, 76, 78, 117, 15,
        105, 89, 11, 95, 86, 101, 115, 25, 38, 91, 92, 125, 107,
    ),
    (
        24, 53, 35, 104, 45, 105, 101, 26, 33, 19, 100, 44, 106, 15, 13, 41, 57, 116, 97, 117, 110, 12, 43,
        56, 55, 61, 125, 123, 60, 21, 75, 84, 70, 94, 114, 2, 73, 50, 52, 77, 14, 7, 32, 5, 39, 92, 38, 22,
        83, 3, 16, 62, 64, 65, 74, 87, 96, 28, 81, 40, 79, 82, 103, 48, 9, 47, 63, 118, 108, 107, 113, 49, 58,
        42, 78, 54, 126, 112, 37, 46, 11, 71, 109, 124, 8, 30, 72, 67, 69, 93, 127, 25, 1, 10, 23, 80, 89,
        115, 4, 98, 59, 90, 88, 95, 111, 27, 29, 18, 31, 76, 86, 122,
    ),
    (
        16, 26, 35, 76, 69, 38, 123, 113, 33, 48, 92, 109, 100, 36, 96, 42, 49, 64, 53, 62, 122, 9, 114, 27,
        68, 97, 117, 101, 11, 105, 75, 29, 81, 94, 19, 65, 41, 59, 83, 89, 14, 6, 8, 24, 90, 87, 86, 126, 111,
        43, 25, 50, 63, 71, 127, 7, 52, 1, 57, 72, 61, 5, 124, 32, 104, 56, 40, 85, 70, 39, 0, 17, 74, 99,
        116, 78, 60, 112, 121, 46, 80, 77, 102, 118, 3, 10, 82, 22, 95, 93, 119, 106, 98, 18, 34, 44, 45, 31,
        120, 2, 58, 66, 108, 125, 103, 12, 4, 91, 51, 79, 84, 110,
    ),
    (
        49, 10, 11, 52, 88, 125, 15, 29, 33, 91, 104, 100, 23, 112, 32, 42, 19, 108, 61, 106, 7, 1, 2, 90, 60,
        21, 86, 78, 24, 30, 58, 84, 13, 110, 47, 31, 25, 59, 46, 38, 118, 83, 8, 48, 40, 64, 53, 74, 39, 3,
        97, 43, 20, 81, 127, 103, 16, 96, 73, 67, 77, 111, 87, 28, 105, 89, 63, 93, 71, 95, 121, 5, 82, 55,
        36, 14, 69, 56, 41, 26, 65, 76, 22, 94, 57, 113, 54, 75, 70, 117, 126, 4, 9, 66, 35, 45, 101, 107,
        120, 98, 6, 27, 79, 92, 122, 44, 37, 50, 99, 116, 109, 124,
    ),
    (
        1, 40, 59, 77, 37, 83, 15, 25, 35, 11, 124, 45, 114, 123, 16, 74, 48, 96, 117, 2, 108, 120, 50, 90,
        84, 85, 30, 4, 33, 113, 43, 55, 46, 62, 70, 65, 57, 58, 79, 69, 18, 111, 8, 26, 34, 87, 28, 31, 67,
        32, 81, 42, 60, 78, 54, 102, 112, 9, 98, 72, 52, 103, 127, 64, 0, 19, 51, 100, 110, 119, 24, 17, 49,
        10, 92, 101, 126, 88, 97, 61, 41, 68, 105, 7, 20, 53, 38, 23, 109, 125, 86, 115, 29, 66, 75, 116, 93,
        71, 56, 13, 91, 3, 76, 21, 22, 27, 122, 82, 63, 95, 94, 118,
    ),
    (
        25, 67, 19, 36, 120, 5, 79, 105, 98, 75, 4, 93, 121, 116, 28, 42, 40, 60, 73, 117, 44, 1, 58, 59, 21,
        69, 99, 115, 8, 9, 123, 80, 82, 122, 71, 2, 97, 57, 64, 109, 118, 103, 112, 18, 10, 104, 52, 86, 23,
        24, 48, 66, 72, 65, 30, 107, 96, 29, 53, 63, 92, 126, 7, 16, 41, 62, 31, 125, 101, 95, 56, 89, 45, 39,
        20, 94, 124, 37, 49, 70, 47, 100, 110, 127, 113, 22, 26, 35, 12, 61, 111, 33, 3, 50, 74, 87, 77, 15,
        11, 32, 14, 43, 108, 84, 78, 27, 88, 38, 83, 76, 54, 6,
    ),
)


def split(x):
    high = x.astype(BF16)
    return high, (x - high.astype(F32)).astype(BF16)


def product(left, right, dims):
    lh, ll = left
    rh, rl = right

    def dot(a, b):
        return lax.dot_general(a, b, (dims, ((), ())), preferred_element_type=F32)

    return dot(lh, rh) + (dot(lh, rl) + dot(ll, rh))


NT = ((1,), (1,))
NN = ((1,), (0,))


def weight_row(info, c):
    c_index = info[2] + c
    d_index = info[3] + lax.broadcasted_iota(jnp.int32, (1, D), 1)
    return jnp.where(c_index < d_index, 1.0, jnp.where(c_index == d_index, 0.5, 0.0)).astype(F32)


def prepare_kernel(info, amp, plus, minus, *refs):
    slots, (kept0, kept1) = refs[: 2 * CHUNKS], refs[2 * CHUNKS : 2 * CHUNKS + 2]
    abuf, wbuf, ibuf, mbuf, sem_in, sem_out = refs[2 * CHUNKS + 2 :]
    role, core = info[0], info[1]

    @pl.when(role != UPPER)
    def _():
        loads = [
            pltpu.make_async_copy(amp.at[:, pl.ds(LOW * g, LOW), :], abuf.at[g], sem_in.at[g])
            for g in range(GROUPS)
        ]
        for load in loads:
            load.start()
        stores = []
        for g in range(GROUPS):
            loads[g].wait()
            rows = abuf.at[g].reshape(PAIRS * LOW, D)

            def step(low, carry, rows=rows, g=g):
                turned = rows[pl.ds(low, PAIRS, stride=LOW), :].T
                for u in range(2):
                    for h in range(2):
                        wbuf[u, h, g, pl.ds(low, C, stride=LOW), :] = turned[
                            C * u : C * u + C, D * h : D * h + D
                        ]
                return carry

            lax.fori_loop(0, LOW, step, 0, unroll=2)
            first = len(stores)
            for j in range(CHUNKS):
                for t in range(2):
                    stores.append(
                        pltpu.make_async_copy(
                            wbuf.at[core ^ t, :, g, pl.ds(WINDOW * LOW * j, SROWS), :],
                            slots[2 * j + t].at[:, pl.ds(SROWS * g, SROWS), :],
                            sem_out.at[len(stores)],
                        )
                    )
                for u, kept in enumerate((kept0, kept1)):
                    stores.append(
                        pltpu.make_async_copy(
                            wbuf.at[u, :, g, pl.ds(WINDOW * LOW * j + SROWS, KROWS), :],
                            kept.at[:, j, g],
                            sem_out.at[len(stores)],
                        )
                    )
            for store in stores[first:]:
                store.start()
        for store in stores:
            store.wait()

    @pl.when(role == UPPER)
    def _():
        loads = [
            [
                pltpu.make_async_copy(
                    ref.at[:, pl.ds(WINDOW * j + 8, 8), :], ibuf.at[i, j], sem_in.at[CHUNKS * i + j]
                )
                for i, ref in enumerate((plus, minus))
            ]
            for j in range(CHUNKS)
        ]
        for pair in loads:
            for load in pair:
                load.start()
        used = 2 * GROUPS * KROWS
        stores = []
        for j in range(CHUNKS):
            for i in range(2):
                loads[j][i].wait()
                rows = ibuf.at[i, j].reshape(PAIRS * 8, D)
                for c in range(KEPT):
                    turned = rows[pl.ds(8 - KEPT + c, PAIRS, stride=8), :].T
                    for l in range(2):
                        for h in range(2):
                            for g in range(GROUPS):
                                mbuf[l, j, h, pl.ds((i * GROUPS + g) * KROWS + c * LOW, LOW), :] = turned[
                                    C * l + LOW * g : C * l + LOW * g + LOW, D * h : D * h + D
                                ]
            for l in range(2):
                for h in range(2):
                    mbuf[l, j, h, pl.ds(used, HALF - used), :] = jnp.zeros((HALF - used, D), F32)
            for t in range(2):
                store = pltpu.make_async_copy(mbuf.at[core ^ t, j], slots[2 * j + t], sem_out.at[len(stores)])
                store.start()
                stores.append(store)
        for store in stores:
            store.wait()


def own_kernel(start, info, plus, minus, amp, kept0, kept1, cross, *refs):
    sym, anti = refs[-2:]
    role, core, block = info[0], info[1], pl.program_id(0) + start

    @pl.when(block == start)
    def _():
        for ref, i in ((sym, 0), (anti, 1)):
            ref[...] = refs[i][...] if start else jnp.zeros_like(ref)

    def taken(ref, low, weighted):
        part = ref.reshape(PAIRS * 8, D)[pl.ds(low, PAIRS, stride=8), :]
        return part * weight_row(info, block * 8 + low) if weighted else part

    @pl.when(role != LOWER)
    def _():
        right = split(jnp.concatenate([taken(amp, low, False) for low in range(8)], axis=1))
        for ref, out in ((plus, sym), (minus, anti)):
            left = split(jnp.concatenate([taken(ref, low, True) for low in range(8)], axis=1))
            out[...] += product(left, right, NT)

    @pl.when((role == DIAG) & (block % 2 == 1))
    def _():
        def rows_of(ref, h, c):
            return [ref[h, 0, g, pl.ds(c * LOW, LOW), :] for g in range(GROUPS)]

        rights = []
        for h in range(2):
            pieces = []
            for c in range(KEPT):
                first = jnp.concatenate(rows_of(kept0, h, c), axis=0)
                pieces.append(jnp.where(core == 0, first, 0.0))
                theirs = jnp.concatenate(rows_of(cross, h, c), axis=0)
                pieces.append(jnp.where(core == 0, theirs, jnp.concatenate(rows_of(kept1, h, c), axis=0)))
            rights.append(jnp.concatenate(pieces, axis=0))
        right = split(jnp.concatenate(rights, axis=1))
        lows = range(8 - KEPT, 8)
        for ref, out, sign in ((plus, sym, 1.0), (minus, anti, -1.0)):
            left = split(jnp.concatenate([taken(ref, low, True) for low in lows], axis=1))
            out[...] += sign * product(left, right, NN)


def mirror_kernel(chunks, info, sym, anti, plus, minus, kept0, kept1, *refs):
    count = len(chunks)
    arrived, outs = refs[: 3 * count], refs[3 * count : -6]
    ibuf, gbuf, kbuf, res, sem_i, sem_g = refs[-6:]
    role, core = info[0], info[1]
    gets = []
    for n in range(count):
        same, other, own = arrived[3 * n : 3 * n + 3]
        get = [
            pltpu.make_async_copy(ref, gbuf.at[n, t], sem_g.at[2 * n + t]) for t, ref in enumerate((same, other))
        ]
        get[1].start()

        @pl.when(role == DIAG)
        def _(n=n, own=own):
            pltpu.make_async_copy(own, gbuf.at[n, 0], sem_g.at[2 * n]).start()

        @pl.when(role != DIAG)
        def _(get=get):
            get[0].start()

        gets.append(get)
    res[0] = sym[...]
    res[1] = anti[...]

    @pl.when(role != LOWER)
    def _():
        loads = [
            [
                [
                    pltpu.make_async_copy(
                        ref.at[:, pl.ds(WINDOW * chunk + 8 * part, 8), :],
                        ibuf.at[n, part, i],
                        sem_i.at[n, 2 * part + i],
                    )
                    for i, ref in enumerate((plus, minus))
                ]
                for part in range(2)
            ]
            for n, chunk in enumerate(chunks)
        ]
        for parts in loads:
            for pair in parts:
                for load in pair:
                    load.start()
        for n, chunk in enumerate(chunks):
            for get in gets[n]:
                get.wait()
            for part in range(2):
                rows_of_c = range(8 * part, min(8 * part + 8, SENT))
                rights = []
                for h in range(2):
                    pieces = []
                    for c in rows_of_c:
                        for l in range(2):
                            for g in range(GROUPS):
                                pieces.append(gbuf[n, core ^ l, h, pl.ds(g * SROWS + c * LOW, LOW), :])
                    rights.append(jnp.concatenate(pieces, axis=0))
                right = split(jnp.concatenate(rights, axis=1))
                for i in range(2):
                    loads[n][part][i].wait()
                    rows = ibuf.at[n, part, i].reshape(PAIRS * 8, D)
                    left = split(
                        jnp.concatenate(
                            [
                                rows[pl.ds(c % 8, PAIRS, stride=8), :] * weight_row(info, WINDOW * chunk + c)
                                for c in rows_of_c
                            ],
                            axis=1,
                        )
                    )
                    gain = product(left, right, NN)
                    res[i] = res[i] + gain if i == 0 else res[i] - gain

    @pl.when(role == LOWER)
    def _():
        loads = [
            [
                pltpu.make_async_copy(ref.at[:, chunk], kbuf.at[n, u], sem_i.at[n, u])
                for u, ref in enumerate((kept0, kept1))
            ]
            for n, chunk in enumerate(chunks)
        ]
        for pair in loads:
            for load in pair:
                load.start()
        rows = GROUPS * KROWS
        for n in range(count):
            for get in gets[n]:
                get.wait()
            for load in loads[n]:
                load.wait()
            right = split(
                jnp.concatenate(
                    [
                        jnp.concatenate([kbuf[n, core ^ t, h].reshape(rows, D) for t in range(2)], axis=0)
                        for h in range(2)
                    ],
                    axis=1,
                )
            )
            for i in range(2):
                left = jnp.concatenate(
                    [
                        jnp.concatenate([gbuf[n, t, h, pl.ds(i * rows, rows), :] for t in range(2)], axis=0).T
                        for h in range(2)
                    ],
                    axis=0,
                )
                gain = product(split(left), right, NN)
                res[i] = res[i] + gain if i == 0 else res[i] - gain

    if CHUNKS - 1 not in chunks:
        outs[0][...] = res[0]
        outs[1][...] = res[1]
    else:
        pack_parts(res, outs[0])


def pack_parts(res, out):
    both = res[0] + res[1], res[0] - res[1]
    res[0] = both[0]
    res[1] = both[1]
    lane = lax.broadcasted_iota(jnp.int32, (8, D), 1) // 32

    def pack(r, carry):
        at = pl.multiple_of(r * 16, 16)
        parts = [res[o, pl.ds(at + 8 * f if f else at, 8), :] for o in range(2) for f in range(2)]
        for k in range(8):
            tile = None
            for g in range(4):
                x = parts[g][:, D * (k // 4) : D * (k // 4) + D]
                shift = (32 * g - 32 * (k % 4)) % D
                x = pltpu.roll(x, shift, 1) if shift else x
                tile = x if tile is None else jnp.where(lane == g, x, tile)
            out[r * 8 + k] = tile
        return carry

    lax.fori_loop(0, 16, pack, 0)


def sum_kernel(parts, upper, lower):
    total = jnp.sum(parts[...], axis=0)
    for g, ref in enumerate((upper, upper, lower, lower)):
        ref[8 * (g % 2) : 8 * (g % 2) + 8, :] = total[:, 32 * g : 32 * g + 32]


def whole(shape):
    return pl.BlockSpec(shape, lambda *_: (0,) * len(shape))


ANY = pl.BlockSpec(memory_space=HBM)
SCALARS = pl.BlockSpec(memory_space=pltpu.SMEM)


def device(row_chip, core, col):
    return (row_chip * 2 + core) * 8 + col


def legs(slot):
    chips = [(r, k) for r in range(8) for k in range(8)]
    senders = sorted(device(r, u, k) for r, k in chips if r != k for u in range(2))
    first, second = [], []
    for source, via in zip(senders, ROUTES[slot]):
        chip, core, col = source // 16, source // 8 % 2, source % 8
        first.append((source, via))
        second.append((via, device(col, core ^ (slot % 2), chip)))
    if slot % 2:
        inside = [(device(r, 1, r), device(r, 0, r)) for r in range(8)]
        first += inside
        second += [(b, b) for _, b in inside]
    return first, second


def body(amplitudes, int_plus, int_minus):
    row, col = lax.axis_index("row"), lax.axis_index("col")
    chip, core = row // 2, row % 2
    role = jnp.where(chip > col, LOWER, jnp.where(chip < col, UPPER, DIAG))
    info = jnp.stack([role, core, row * C, col * D]).astype(jnp.int32)

    slot_shape = jax.ShapeDtypeStruct((2, HALF, D), F32)
    kept_shape = jax.ShapeDtypeStruct((2, CHUNKS, GROUPS, KROWS, D), F32)
    *slots, kept0, kept1 = pl.pallas_call(
        prepare_kernel,
        in_specs=[SCALARS, ANY, ANY, ANY],
        out_specs=[ANY] * (2 * CHUNKS + 2),
        out_shape=[slot_shape] * (2 * CHUNKS) + [kept_shape] * 2,
        scratch_shapes=[
            pltpu.VMEM((GROUPS, PAIRS, LOW, D), F32),
            pltpu.VMEM((2, 2, GROUPS, C * LOW, D), F32),
            pltpu.VMEM((2, CHUNKS, PAIRS, 8, D), F32),
            pltpu.VMEM((2, CHUNKS, 2, HALF, D), F32),
            pltpu.SemaphoreType.DMA((2 * CHUNKS,)),
            pltpu.SemaphoreType.DMA((64,)),
        ],
        name="prepare",
    )(info, amplitudes, int_plus, int_minus)

    ways = [legs(slot) for slot in range(2 * CHUNKS)]
    passing = [lax.ppermute(x, AXES, way[0]) for x, way in zip(slots, ways)]
    cross = lax.ppermute(kept0, AXES, [(device(r, 1, r), device(r, 0, r)) for r in range(8)])
    square = jax.ShapeDtypeStruct((PAIRS, PAIRS), F32)

    def own_part(start, stop, plus, sums):
        def at(j, info):
            return jnp.where(info[0] == LOWER, 0, j + start)

        block = pl.BlockSpec((PAIRS, 8, D), lambda j, info: (0, at(j, info), 0))
        kept_block = pl.BlockSpec(
            (2, 1, GROUPS, KROWS, D),
            lambda j, info: (0, jnp.where(info[0] == DIAG, (j + start) // 2, 0), 0, 0, 0),
        )
        return pl.pallas_call(
            partial(own_kernel, start),
            grid_spec=pltpu.PrefetchScalarGridSpec(
                num_scalar_prefetch=1,
                grid=(stop - start,),
                in_specs=[block] * 3 + [kept_block] * 3 + [whole((PAIRS, PAIRS))] * len(sums),
                out_specs=[whole((PAIRS, PAIRS))] * 2,
            ),
            out_shape=[square] * 2,
            compiler_params=pltpu.CompilerParams(dimension_semantics=("arbitrary",)),
            name=f"own{start}",
        )(info, plus, int_minus, amplitudes, kept0, kept1, cross, *sums)

    sums = ()
    for (start, stop), slot in OWN:
        plus = lax.optimization_barrier((int_plus, passing[slot - 1]))[0] if slot else int_plus
        sums = own_part(start, stop, plus, sums)
        for s in range(slot, 2 * CHUNKS):
            passing[s] = lax.optimization_barrier((passing[s], sums[0]))[0]
    sym, anti = sums
    got = [lax.ppermute(x, AXES, way[1]) for x, way in zip(passing, ways)]

    for chunks in MIRROR:
        last = CHUNKS - 1 in chunks
        count = len(chunks)
        packed = jax.ShapeDtypeStruct((128, 8, D), F32)
        out = pl.pallas_call(
            partial(mirror_kernel, chunks),
            in_specs=[SCALARS, whole((PAIRS, PAIRS)), whole((PAIRS, PAIRS))] + [ANY] * (4 + 3 * count),
            out_specs=[whole((128, 8, D))] if last else [whole((PAIRS, PAIRS))] * 2,
            out_shape=[packed] if last else [square] * 2,
            scratch_shapes=[
                pltpu.VMEM((count, 2, 2, PAIRS, 8, D), F32),
                pltpu.VMEM((count, 2, 2, HALF, D), F32),
                pltpu.VMEM((count, 2, 2, GROUPS, KROWS, D), F32),
                pltpu.VMEM((2, PAIRS, PAIRS), F32),
                pltpu.SemaphoreType.DMA((count, 4)),
                pltpu.SemaphoreType.DMA((2 * count,)),
            ],
            name=f"mirror{chunks[0]}",
        )(
            info, sym, anti, int_plus, int_minus, kept0, kept1,
            *(x for j in chunks for x in (got[2 * j], got[2 * j + 1], slots[2 * j])),
        )
        if not last:
            sym, anti = out

    parts = lax.all_to_all(out[0], AXES, 0, 0, tiled=True)
    return pl.pallas_call(
        sum_kernel,
        in_specs=[whole((128, 8, D))],
        out_specs=[whole((16, 32))] * 2,
        out_shape=[jax.ShapeDtypeStruct((16, 32), F32)] * 2,
        grid=(1,),
        name="total",
    )(parts)


def solution(mesh):
    spec = P(None, "row", "col")
    out = (P("row", "col"), P("row", "col"))
    return jax.shard_map(body, mesh=mesh, in_specs=(spec,) * 3, out_specs=out, check_vma=False)
```

```python
from functools import partial

import jax
import jax.numpy as jnp
from jax import lax
from jax.experimental import pallas as pl
from jax.experimental.pallas import tpu as pltpu
from jax.sharding import PartitionSpec as P

AXES = ("row", "col")
F32 = jnp.float32
BF16 = jnp.bfloat16


PAIRS, C, D = 256, 64, 128
CHUNKS, WINDOW = 4, 16
SENT, KEPT = 11, 5
GROUPS, LOW = 4, 16
SROWS, KROWS = SENT * LOW, KEPT * LOW
HALF = GROUPS * SROWS
LOWER, UPPER, DIAG = 0, 1, 2
MIRROR = ((0, 1), (2, 3))
OWN = (((0, 4), 0), ((4, 8), 4))
HBM = pltpu.MemorySpace.HBM

ROUTES = (
    (
        19, 40, 59, 37, 113, 30, 100, 17, 10, 55, 80, 46, 31, 99, 3, 38, 51, 92, 29, 126, 110, 112, 58, 4,
        106, 68, 122, 15, 33, 25, 50, 63, 45, 94, 91, 8, 57, 56, 88, 70, 119, 121, 9, 18, 43, 95, 76, 127,
        107, 24, 26, 42, 75, 89, 74, 1, 48, 0, 90, 32, 81, 102, 108, 96, 41, 47, 35, 86, 103, 125, 16, 5, 49,
        34, 84, 78, 67, 123, 61, 62, 64, 72, 117, 87, 115, 13, 22, 2, 79, 101, 116, 114, 11, 82, 60, 71, 69,
        109, 28, 98, 6, 7, 77, 93, 111, 120, 20, 14, 27, 124, 85, 118,
    ),
    (
        5, 40, 38, 71, 90, 120, 123, 10, 42, 3, 93, 109, 127, 111, 9, 11, 18, 52, 125, 107, 28, 1, 62, 47, 96,
        101, 118, 103, 20, 19, 55, 79, 89, 6, 7, 2, 13, 54, 39, 48, 126, 82, 12, 57, 46, 74, 37, 22, 75, 32,
        56, 58, 72, 77, 86, 104, 60, 33, 67, 95, 81, 78, 115, 25, 105, 50, 63, 65, 83, 100, 27, 61, 45, 43,
        92, 117, 116, 14, 121, 49, 44, 69, 122, 98, 24, 97, 30, 66, 70, 73, 124, 15, 21, 41, 23, 76, 94, 99,
        16, 4, 80, 35, 64, 87, 110, 112, 8, 26, 59, 108, 84, 106,
    ),
    (
        17, 41, 35, 116, 79, 121, 4, 24, 34, 50, 124, 68, 114, 123, 0, 26, 56, 97, 81, 98, 22, 28, 62, 57, 64,
        69, 30, 120, 8, 2, 40, 73, 93, 102, 108, 3, 1, 59, 85, 90, 13, 83, 16, 49, 43, 60, 80, 29, 20, 19, 27,
        33, 87, 70, 31, 103, 32, 9, 53, 94, 84, 109, 127, 44, 99, 54, 52, 37, 110, 63, 48, 112, 36, 47, 88,
        111, 106, 18, 72, 46, 51, 77, 126, 119, 5, 10, 58, 75, 100, 71, 118, 12, 21, 74, 42, 76, 78, 117, 15,
        105, 89, 11, 95, 86, 101, 115, 25, 38, 91, 92, 125, 107,
    ),
    (
        24, 53, 35, 104, 45, 105, 101, 26, 33, 19, 100, 44, 106, 15, 13, 41, 57, 116, 97, 117, 110, 12, 43,
        56, 55, 61, 125, 123, 60, 21, 75, 84, 70, 94, 114, 2, 73, 50, 52, 77, 14, 7, 32, 5, 39, 92, 38, 22,
        83, 3, 16, 62, 64, 65, 74, 87, 96, 28, 81, 40, 79, 82, 103, 48, 9, 47, 63, 118, 108, 107, 113, 49, 58,
        42, 78, 54, 126, 112, 37, 46, 11, 71, 109, 124, 8, 30, 72, 67, 69, 93, 127, 25, 1, 10, 23, 80, 89,
        115, 4, 98, 59, 90, 88, 95, 111, 27, 29, 18, 31, 76, 86, 122,
    ),
    (
        16, 26, 35, 76, 69, 38, 123, 113, 33, 48, 92, 109, 100, 36, 96, 42, 49, 64, 53, 62, 122, 9, 114, 27,
        68, 97, 117, 101, 11, 105, 75, 29, 81, 94, 19, 65, 41, 59, 83, 89, 14, 6, 8, 24, 90, 87, 86, 126, 111,
        43, 25, 50, 63, 71, 127, 7, 52, 1, 57, 72, 61, 5, 124, 32, 104, 56, 40, 85, 70, 39, 0, 17, 74, 99,
        116, 78, 60, 112, 121, 46, 80, 77, 102, 118, 3, 10, 82, 22, 95, 93, 119, 106, 98, 18, 34, 44, 45, 31,
        120, 2, 58, 66, 108, 125, 103, 12, 4, 91, 51, 79, 84, 110,
    ),
    (
        49, 10, 11, 52, 88, 125, 15, 29, 33, 91, 104, 100, 23, 112, 32, 42, 19, 108, 61, 106, 7, 1, 2, 90, 60,
        21, 86, 78, 24, 30, 58, 84, 13, 110, 47, 31, 25, 59, 46, 38, 118, 83, 8, 48, 40, 64, 53, 74, 39, 3,
        97, 43, 20, 81, 127, 103, 16, 96, 73, 67, 77, 111, 87, 28, 105, 89, 63, 93, 71, 95, 121, 5, 82, 55,
        36, 14, 69, 56, 41, 26, 65, 76, 22, 94, 57, 113, 54, 75, 70, 117, 126, 4, 9, 66, 35, 45, 101, 107,
        120, 98, 6, 27, 79, 92, 122, 44, 37, 50, 99, 116, 109, 124,
    ),
    (
        1, 40, 59, 77, 37, 83, 15, 25, 35, 11, 124, 45, 114, 123, 16, 74, 48, 96, 117, 2, 108, 120, 50, 90,
        84, 85, 30, 4, 33, 113, 43, 55, 46, 62, 70, 65, 57, 58, 79, 69, 18, 111, 8, 26, 34, 87, 28, 31, 67,
        32, 81, 42, 60, 78, 54, 102, 112, 9, 98, 72, 52, 103, 127, 64, 0, 19, 51, 100, 110, 119, 24, 17, 49,
        10, 92, 101, 126, 88, 97, 61, 41, 68, 105, 7, 20, 53, 38, 23, 109, 125, 86, 115, 29, 66, 75, 116, 93,
        71, 56, 13, 91, 3, 76, 21, 22, 27, 122, 82, 63, 95, 94, 118,
    ),
    (
        25, 67, 19, 36, 120, 5, 79, 105, 98, 75, 4, 93, 121, 116, 28, 42, 40, 60, 73, 117, 44, 1, 58, 59, 21,
        69, 99, 115, 8, 9, 123, 80, 82, 122, 71, 2, 97, 57, 64, 109, 118, 103, 112, 18, 10, 104, 52, 86, 23,
        24, 48, 66, 72, 65, 30, 107, 96, 29, 53, 63, 92, 126, 7, 16, 41, 62, 31, 125, 101, 95, 56, 89, 45, 39,
        20, 94, 124, 37, 49, 70, 47, 100, 110, 127, 113, 22, 26, 35, 12, 61, 111, 33, 3, 50, 74, 87, 77, 15,
        11, 32, 14, 43, 108, 84, 78, 27, 88, 38, 83, 76, 54, 6,
    ),
)


def split(x):
    high = x.astype(BF16)
    return high, (x - high.astype(F32)).astype(BF16)


def product(left, right, dims):
    lh, ll = left
    rh, rl = right

    def dot(a, b):
        return lax.dot_general(a, b, (dims, ((), ())), preferred_element_type=F32)

    return dot(lh, rh) + (dot(lh, rl) + dot(ll, rh))


NT = ((1,), (1,))
NN = ((1,), (0,))


def weight_row(info, c):
    c_index = info[2] + c
    d_index = info[3] + lax.broadcasted_iota(jnp.int32, (1, D), 1)
    return jnp.where(c_index < d_index, 1.0, jnp.where(c_index == d_index, 0.5, 0.0)).astype(F32)


def prepare_kernel(info, amp, plus, minus, *refs):
    slots, (kept0, kept1) = refs[: 2 * CHUNKS], refs[2 * CHUNKS : 2 * CHUNKS + 2]
    abuf, wbuf, ibuf, mbuf, sem_in, sem_out = refs[2 * CHUNKS + 2 :]
    role, core = info[0], info[1]

    @pl.when(role != UPPER)
    def _():
        loads = [
            pltpu.make_async_copy(amp.at[:, pl.ds(LOW * g, LOW), :], abuf.at[g], sem_in.at[g])
            for g in range(GROUPS)
        ]
        for load in loads:
            load.start()
        stores = []
        for g in range(GROUPS):
            loads[g].wait()
            rows = abuf.at[g].reshape(PAIRS * LOW, D)

            def step(low, carry, rows=rows, g=g):
                turned = rows[pl.ds(low, PAIRS, stride=LOW), :].T
                for u in range(2):
                    for h in range(2):
                        wbuf[u, h, g, pl.ds(low, C, stride=LOW), :] = turned[
                            C * u : C * u + C, D * h : D * h + D
                        ]
                return carry

            lax.fori_loop(0, LOW, step, 0, unroll=2)
            first = len(stores)
            for j in range(CHUNKS):
                for t in range(2):
                    stores.append(
                        pltpu.make_async_copy(
                            wbuf.at[core ^ t, :, g, pl.ds(WINDOW * LOW * j, SROWS), :],
                            slots[2 * j + t].at[:, pl.ds(SROWS * g, SROWS), :],
                            sem_out.at[len(stores)],
                        )
                    )
                for u, kept in enumerate((kept0, kept1)):
                    stores.append(
                        pltpu.make_async_copy(
                            wbuf.at[u, :, g, pl.ds(WINDOW * LOW * j + SROWS, KROWS), :],
                            kept.at[:, j, g],
                            sem_out.at[len(stores)],
                        )
                    )
            for store in stores[first:]:
                store.start()
        for store in stores:
            store.wait()

    @pl.when(role == UPPER)
    def _():
        loads = [
            [
                pltpu.make_async_copy(
                    ref.at[:, pl.ds(WINDOW * j + 8, 8), :], ibuf.at[i, j], sem_in.at[CHUNKS * i + j]
                )
                for i, ref in enumerate((plus, minus))
            ]
            for j in range(CHUNKS)
        ]
        for pair in loads:
            for load in pair:
                load.start()
        used = 2 * GROUPS * KROWS
        stores = []
        for j in range(CHUNKS):
            for i in range(2):
                loads[j][i].wait()
                rows = ibuf.at[i, j].reshape(PAIRS * 8, D)
                for c in range(KEPT):
                    turned = rows[pl.ds(8 - KEPT + c, PAIRS, stride=8), :].T
                    for l in range(2):
                        for h in range(2):
                            for g in range(GROUPS):
                                mbuf[l, j, h, pl.ds((i * GROUPS + g) * KROWS + c * LOW, LOW), :] = turned[
                                    C * l + LOW * g : C * l + LOW * g + LOW, D * h : D * h + D
                                ]
            for l in range(2):
                for h in range(2):
                    mbuf[l, j, h, pl.ds(used, HALF - used), :] = jnp.zeros((HALF - used, D), F32)
            for t in range(2):
                store = pltpu.make_async_copy(mbuf.at[core ^ t, j], slots[2 * j + t], sem_out.at[len(stores)])
                store.start()
                stores.append(store)
        for store in stores:
            store.wait()


def own_kernel(start, info, plus, minus, amp, kept0, kept1, cross, *refs):
    sym, anti = refs[-2:]
    role, core, block = info[0], info[1], pl.program_id(0) + start

    @pl.when(block == start)
    def _():
        for ref, i in ((sym, 0), (anti, 1)):
            ref[...] = refs[i][...] if start else jnp.zeros_like(ref)

    def taken(ref, low, weighted):
        part = ref.reshape(PAIRS * 8, D)[pl.ds(low, PAIRS, stride=8), :]
        return part * weight_row(info, block * 8 + low) if weighted else part

    @pl.when(role != LOWER)
    def _():
        right = split(jnp.concatenate([taken(amp, low, False) for low in range(8)], axis=1))
        for ref, out in ((plus, sym), (minus, anti)):
            left = split(jnp.concatenate([taken(ref, low, True) for low in range(8)], axis=1))
            out[...] += product(left, right, NT)

    @pl.when((role == DIAG) & (block % 2 == 1))
    def _():
        def rows_of(ref, h, c):
            return [ref[h, 0, g, pl.ds(c * LOW, LOW), :] for g in range(GROUPS)]

        rights = []
        for h in range(2):
            pieces = []
            for c in range(KEPT):
                first = jnp.concatenate(rows_of(kept0, h, c), axis=0)
                pieces.append(jnp.where(core == 0, first, 0.0))
                theirs = jnp.concatenate(rows_of(cross, h, c), axis=0)
                pieces.append(jnp.where(core == 0, theirs, jnp.concatenate(rows_of(kept1, h, c), axis=0)))
            rights.append(jnp.concatenate(pieces, axis=0))
        right = split(jnp.concatenate(rights, axis=1))
        lows = range(8 - KEPT, 8)
        for ref, out, sign in ((plus, sym, 1.0), (minus, anti, -1.0)):
            left = split(jnp.concatenate([taken(ref, low, True) for low in lows], axis=1))
            out[...] += sign * product(left, right, NN)


def mirror_kernel(chunks, info, sym, anti, plus, minus, kept0, kept1, *refs):
    count = len(chunks)
    arrived, outs = refs[: 3 * count], refs[3 * count : -6]
    ibuf, gbuf, kbuf, res, sem_i, sem_g = refs[-6:]
    role, core = info[0], info[1]
    gets = []
    for n in range(count):
        same, other, own = arrived[3 * n : 3 * n + 3]
        get = [
            pltpu.make_async_copy(ref, gbuf.at[n, t], sem_g.at[2 * n + t]) for t, ref in enumerate((same, other))
        ]
        get[1].start()

        @pl.when(role == DIAG)
        def _(n=n, own=own):
            pltpu.make_async_copy(own, gbuf.at[n, 0], sem_g.at[2 * n]).start()

        @pl.when(role != DIAG)
        def _(get=get):
            get[0].start()

        gets.append(get)
    res[0] = sym[...]
    res[1] = anti[...]

    @pl.when(role != LOWER)
    def _():
        loads = [
            [
                [
                    pltpu.make_async_copy(
                        ref.at[:, pl.ds(WINDOW * chunk + 8 * part, 8), :],
                        ibuf.at[n, part, i],
                        sem_i.at[n, 2 * part + i],
                    )
                    for i, ref in enumerate((plus, minus))
                ]
                for part in range(2)
            ]
            for n, chunk in enumerate(chunks)
        ]
        for parts in loads:
            for pair in parts:
                for load in pair:
                    load.start()
        for n, chunk in enumerate(chunks):
            for get in gets[n]:
                get.wait()
            for part in range(2):
                rows_of_c = range(8 * part, min(8 * part + 8, SENT))
                rights = []
                for h in range(2):
                    pieces = []
                    for c in rows_of_c:
                        for l in range(2):
                            for g in range(GROUPS):
                                pieces.append(gbuf[n, core ^ l, h, pl.ds(g * SROWS + c * LOW, LOW), :])
                    rights.append(jnp.concatenate(pieces, axis=0))
                right = split(jnp.concatenate(rights, axis=1))
                for i in range(2):
                    loads[n][part][i].wait()
                    rows = ibuf.at[n, part, i].reshape(PAIRS * 8, D)
                    left = split(
                        jnp.concatenate(
                            [
                                rows[pl.ds(c % 8, PAIRS, stride=8), :] * weight_row(info, WINDOW * chunk + c)
                                for c in rows_of_c
                            ],
                            axis=1,
                        )
                    )
                    gain = product(left, right, NN)
                    res[i] = res[i] + gain if i == 0 else res[i] - gain

    @pl.when(role == LOWER)
    def _():
        loads = [
            [
                pltpu.make_async_copy(ref.at[:, chunk], kbuf.at[n, u], sem_i.at[n, u])
                for u, ref in enumerate((kept0, kept1))
            ]
            for n, chunk in enumerate(chunks)
        ]
        for pair in loads:
            for load in pair:
                load.start()
        rows = GROUPS * KROWS
        for n in range(count):
            for get in gets[n]:
                get.wait()
            for load in loads[n]:
                load.wait()
            right = split(
                jnp.concatenate(
                    [
                        jnp.concatenate([kbuf[n, core ^ t, h].reshape(rows, D) for t in range(2)], axis=0)
                        for h in range(2)
                    ],
                    axis=1,
                )
            )
            for i in range(2):
                left = jnp.concatenate(
                    [
                        jnp.concatenate([gbuf[n, t, h, pl.ds(i * rows, rows), :] for t in range(2)], axis=0).T
                        for h in range(2)
                    ],
                    axis=0,
                )
                gain = product(split(left), right, NN)
                res[i] = res[i] + gain if i == 0 else res[i] - gain

    if CHUNKS - 1 not in chunks:
        outs[0][...] = res[0]
        outs[1][...] = res[1]
    else:
        pack_parts(res, outs[0])


def pack_parts(res, out):
    both = res[0] + res[1], res[0] - res[1]
    res[0] = both[0]
    res[1] = both[1]
    lane = lax.broadcasted_iota(jnp.int32, (8, D), 1) // 32

    def pack(r, carry):
        at = pl.multiple_of(r * 16, 16)
        parts = [res[o, pl.ds(at + 8 * f if f else at, 8), :] for o in range(2) for f in range(2)]
        for k in range(8):
            tile = None
            for g in range(4):
                x = parts[g][:, D * (k // 4) : D * (k // 4) + D]
                shift = (32 * g - 32 * (k % 4)) % D
                x = pltpu.roll(x, shift, 1) if shift else x
                tile = x if tile is None else jnp.where(lane == g, x, tile)
            out[r * 8 + k] = tile
        return carry

    lax.fori_loop(0, 16, pack, 0)


def sum_kernel(parts, upper, lower):
    total = jnp.sum(parts[...], axis=0)
    for g, ref in enumerate((upper, upper, lower, lower)):
        ref[8 * (g % 2) : 8 * (g % 2) + 8, :] = total[:, 32 * g : 32 * g + 32]


def whole(shape):
    return pl.BlockSpec(shape, lambda *_: (0,) * len(shape))


ANY = pl.BlockSpec(memory_space=HBM)
SCALARS = pl.BlockSpec(memory_space=pltpu.SMEM)


def device(row_chip, core, col):
    return (row_chip * 2 + core) * 8 + col


def legs(slot):
    chips = [(r, k) for r in range(8) for k in range(8)]
    senders = sorted(device(r, u, k) for r, k in chips if r != k for u in range(2))
    first, second = [], []
    for source, via in zip(senders, ROUTES[slot]):
        chip, core, col = source // 16, source // 8 % 2, source % 8
        first.append((source, via))
        second.append((via, device(col, core ^ (slot % 2), chip)))
    if slot % 2:
        inside = [(device(r, 1, r), device(r, 0, r)) for r in range(8)]
        first += inside
        second += [(b, b) for _, b in inside]
    return first, second


def body(amplitudes, int_plus, int_minus):
    row, col = lax.axis_index("row"), lax.axis_index("col")
    chip, core = row // 2, row % 2
    role = jnp.where(chip > col, LOWER, jnp.where(chip < col, UPPER, DIAG))
    info = jnp.stack([role, core, row * C, col * D]).astype(jnp.int32)

    slot_shape = jax.ShapeDtypeStruct((2, HALF, D), F32)
    kept_shape = jax.ShapeDtypeStruct((2, CHUNKS, GROUPS, KROWS, D), F32)
    *slots, kept0, kept1 = pl.pallas_call(
        prepare_kernel,
        in_specs=[SCALARS, ANY, ANY, ANY],
        out_specs=[ANY] * (2 * CHUNKS + 2),
        out_shape=[slot_shape] * (2 * CHUNKS) + [kept_shape] * 2,
        scratch_shapes=[
            pltpu.VMEM((GROUPS, PAIRS, LOW, D), F32),
            pltpu.VMEM((2, 2, GROUPS, C * LOW, D), F32),
            pltpu.VMEM((2, CHUNKS, PAIRS, 8, D), F32),
            pltpu.VMEM((2, CHUNKS, 2, HALF, D), F32),
            pltpu.SemaphoreType.DMA((2 * CHUNKS,)),
            pltpu.SemaphoreType.DMA((64,)),
        ],
        name="prepare",
    )(info, amplitudes, int_plus, int_minus)

    ways = [legs(slot) for slot in range(2 * CHUNKS)]
    passing = [lax.ppermute(x, AXES, way[0]) for x, way in zip(slots, ways)]
    cross = lax.ppermute(kept0, AXES, [(device(r, 1, r), device(r, 0, r)) for r in range(8)])
    square = jax.ShapeDtypeStruct((PAIRS, PAIRS), F32)

    def own_part(start, stop, plus, sums):
        def at(j, info):
            return jnp.where(info[0] == LOWER, 0, j + start)

        block = pl.BlockSpec((PAIRS, 8, D), lambda j, info: (0, at(j, info), 0))
        kept_block = pl.BlockSpec(
            (2, 1, GROUPS, KROWS, D),
            lambda j, info: (0, jnp.where(info[0] == DIAG, (j + start) // 2, 0), 0, 0, 0),
        )
        return pl.pallas_call(
            partial(own_kernel, start),
            grid_spec=pltpu.PrefetchScalarGridSpec(
                num_scalar_prefetch=1,
                grid=(stop - start,),
                in_specs=[block] * 3 + [kept_block] * 3 + [whole((PAIRS, PAIRS))] * len(sums),
                out_specs=[whole((PAIRS, PAIRS))] * 2,
            ),
            out_shape=[square] * 2,
            compiler_params=pltpu.CompilerParams(dimension_semantics=("arbitrary",)),
            name=f"own{start}",
        )(info, plus, int_minus, amplitudes, kept0, kept1, cross, *sums)

    sums = ()
    for (start, stop), slot in OWN:
        plus = lax.optimization_barrier((int_plus, passing[slot - 1]))[0] if slot else int_plus
        sums = own_part(start, stop, plus, sums)
        for s in range(slot, 2 * CHUNKS):
            passing[s] = lax.optimization_barrier((passing[s], sums[0]))[0]
    sym, anti = sums
    got = [lax.ppermute(x, AXES, way[1]) for x, way in zip(passing, ways)]

    for chunks in MIRROR:
        last = CHUNKS - 1 in chunks
        count = len(chunks)
        packed = jax.ShapeDtypeStruct((128, 8, D), F32)
        out = pl.pallas_call(
            partial(mirror_kernel, chunks),
            in_specs=[SCALARS, whole((PAIRS, PAIRS)), whole((PAIRS, PAIRS))] + [ANY] * (4 + 3 * count),
            out_specs=[whole((128, 8, D))] if last else [whole((PAIRS, PAIRS))] * 2,
            out_shape=[packed] if last else [square] * 2,
            scratch_shapes=[
                pltpu.VMEM((count, 2, 2, PAIRS, 8, D), F32),
                pltpu.VMEM((count, 2, 2, HALF, D), F32),
                pltpu.VMEM((count, 2, 2, GROUPS, KROWS, D), F32),
                pltpu.VMEM((2, PAIRS, PAIRS), F32),
                pltpu.SemaphoreType.DMA((count, 4)),
                pltpu.SemaphoreType.DMA((2 * count,)),
            ],
            name=f"mirror{chunks[0]}",
        )(
            info, sym, anti, int_plus, int_minus, kept0, kept1,
            *(x for j in chunks for x in (got[2 * j], got[2 * j + 1], slots[2 * j])),
        )
        if not last:
            sym, anti = out

    parts = lax.all_to_all(out[0], AXES, 0, 0, tiled=True)
    return pl.pallas_call(
        sum_kernel,
        in_specs=[whole((128, 8, D))],
        out_specs=[whole((16, 32))] * 2,
        out_shape=[jax.ShapeDtypeStruct((16, 32), F32)] * 2,
        grid=(1,),
        name="total",
    )(parts)


def solution(mesh):
    spec = P(None, "row", "col")
    out = (P("row", "col"), P("row", "col"))
    return jax.shard_map(body, mesh=mesh, in_specs=(spec,) * 3, out_specs=out, check_vma=False)
```
